1024 devices in a mesh: wide: 64 (over z_lo, y), narrow: 16 (over x, z_hi, core).
Axes of the slice: x: 4, y: 4, z: 32 (z_hi: 2, z_lo: 16; z = z_hi * 16 + z_lo), core: 2. Of those that a mesh axis runs over, the one named last changes fastest.
Arguments:
- chemical_fractions: float32 [53, 128, 128, 128], P(None, 'wide', 'narrow'), may hold values from 0.1 to 1
- thermal_state: float32 [128, 128, 128], P('wide', 'narrow'), may hold values from 1 to 3
- ignited_stacks: int32 [128, 128], P('wide', 'narrow'), may hold values from 0 to 1, as said below
- spreading_number: float32 [53], replicated, may hold values from 0.02 to 0.15
- natural_exponent_scale: float32 [325], replicated, may hold values from -1 to 1
- arrhenius_energy: float32 [325], replicated, may hold values from 0.5 to 2
- incoming_stoichiometry: int32 [325, 53], replicated, may hold values 0 or 1
- outgoing_stoichiometry: int32 [325, 53], replicated, may hold values 0 or 1
Outputs:
- updated: float32 [53, 128, 128, 128], P(None, 'wide', 'narrow')
The draws below stay inside these ranges and needn't reach their ends.
Inputs may be any that keep to these rules, and one draw needn't show every extreme that they name: `ignited_stacks`: on each device either 8 or 2 of its columns burn. In every group of devices along narrow, those with 8 burning columns are a quarter of the group and consecutive in index, with wrap-around.
All inputs are finite; a program needn't handle non-finite values.
Results may differ from the reference program's by a relative error of at most 0.0001.
Values sent between devices are 32-bit elements; how exact they have to be, the bound alone decides.
No kernel may reach another device: no remote copies, remote signals or barrier semaphores. Data moves between devices by JAX's collectives and lax.ppermute only.
A program may use at most 32 MiB of HBM per device.

```python
import math
import jax
import jax.numpy as jnp
from jax import lax

S = 53
R = 325
CX = 2
CY = 8
STACK_HEIGHT = 128
BURN_MAX = 8
MESH_LEADING = 128
MESH_TRAILING = 128
N_WIDE = 64
N_NARROW = 16


def draw_ignited_stacks(key, part):
    key_rank = jax.random.fold_in(key, 11)
    key_turn = jax.random.fold_in(key, 12)
    stack_total = CX * CY
    scores = jax.random.randint(key_rank, (N_WIDE, N_NARROW, stack_total), 0, 2 ** 20) * stack_total + jnp.arange(stack_total, dtype=jnp.int32)
    order = jnp.argsort(scores, axis=-1)
    ranks = jnp.argsort(order, axis=-1)
    turns = jax.random.randint(key_turn, (N_WIDE, 1), 0, N_NARROW)
    where_at = (jnp.arange(N_NARROW, dtype=jnp.int32)[None, :] + turns) % N_NARROW
    counts = jnp.where(where_at < N_NARROW // 4, BURN_MAX, BURN_MAX // 4)
    marks = (ranks < counts[:, :, None]).astype(jnp.int32)
    marks = marks.reshape(N_WIDE, N_NARROW, CX, CY)
    marks = jnp.transpose(marks, (0, 2, 1, 3))
    return marks.reshape(N_WIDE * CX, N_NARROW * CY)


def place_ends(array, key, least, high):
    shape = array.shape
    place = [jax.random.randint(jax.random.fold_in(key, axis), (), 0, shape[axis]) for axis in range(len(shape))]
    array = array.at[tuple(place)].set(least)
    longest = shape.index(max(shape))
    place[longest] = (place[longest] + 1) % shape[longest]
    return array.at[tuple(place)].set(high)


def shard_levels(stream_key, dims, pieces, least, high):
    level, own = 1.0, jax.random.fold_in(stream_key, 6)
    for axis_at, shards_of in pieces:
        draws = jnp.exp(jax.random.uniform(jax.random.fold_in(own, axis_at), (shards_of,), jnp.float32, least / len(pieces), high / len(pieces)))
        level = level * jnp.repeat(draws, dims[axis_at] // shards_of).reshape([-1 if axis == axis_at else 1 for axis in range(len(dims))])
    return level


def setup_inputs(seed: int = 0) -> dict:
    streams_of = jax.random.split(jax.random.key(seed), 9)
    return {
        "chemical_fractions": jnp.clip(jnp.exp(math.log(1.0) - 2.3025851 * jax.random.uniform(streams_of[0], (S, MESH_LEADING, MESH_TRAILING, STACK_HEIGHT), jnp.float32) ** shard_levels(streams_of[0], (S, MESH_LEADING, MESH_TRAILING, STACK_HEIGHT), ((1, 64), (2, 16)), -0.2, 0.2)), 0.1, 1.0),
        "thermal_state": jnp.clip(1.0 + 2.0 * jax.random.uniform(streams_of[1], (MESH_LEADING, MESH_TRAILING, STACK_HEIGHT), jnp.float32) ** shard_levels(streams_of[1], (MESH_LEADING, MESH_TRAILING, STACK_HEIGHT), ((0, 64), (1, 16)), -0.2, 0.2), 1.0, 3.0),
        "ignited_stacks": draw_ignited_stacks(jax.random.fold_in(streams_of[8], 71), 0),
        "spreading_number": jnp.clip(jax.random.uniform(streams_of[3], (S,), jnp.float32, 0.02, 0.15), 0.02, 0.15),
        "natural_exponent_scale": jnp.clip(jax.random.uniform(streams_of[4], (R,), jnp.float32, -1.0, 1.0), -1.0, 1.0),
        "arrhenius_energy": jnp.clip(jax.random.uniform(streams_of[5], (R,), jnp.float32, 0.5, 2.0), 0.5, 2.0),
        "incoming_stoichiometry": place_ends((jax.random.randint(streams_of[6], (R, S), 0, 20) < 1).astype(jnp.int32), jax.random.fold_in(streams_of[6], 1), 0, 1),
        "outgoing_stoichiometry": place_ends((jax.random.randint(streams_of[7], (R, S), 0, 20) < 1).astype(jnp.int32), jax.random.fold_in(streams_of[7], 1), 0, 1),
    }


def diffuse(fields, coeff):
    beside = jnp.roll(fields, -1, 1) + jnp.roll(fields, 1, 1)
    beside = beside + jnp.roll(fields, -1, 2) + jnp.roll(fields, 1, 2)
    beside = beside + jnp.roll(fields, -1, 3) + jnp.roll(fields, 1, 3)
    return fields + coeff * (beside - 6.0 * fields)


def react(values, enthalpy_output, natural_exponent_scale, arrhenius_energy, react_mat, react_tr, prod_tr):
    for substep in range(2):
        logs = jnp.log(values)
        expo = natural_exponent_scale[:, None] - arrhenius_energy[:, None] / enthalpy_output[None, :] + jnp.dot(react_mat, logs, precision=lax.Precision.HIGHEST, preferred_element_type=jnp.float32)
        rates = jnp.exp(expo)
        gain = jnp.dot(prod_tr, rates, precision=lax.Precision.HIGHEST, preferred_element_type=jnp.float32)
        loss = jnp.dot(react_tr, rates, precision=lax.Precision.HIGHEST, preferred_element_type=jnp.float32)
        values = values * (values + 0.5 * gain) / (values + 0.5 * loss)
    return values


def reference(chemical_fractions, thermal_state, ignited_stacks, spreading_number, natural_exponent_scale, arrhenius_energy, incoming_stoichiometry, outgoing_stoichiometry):
    coeff = spreading_number[:, None, None, None]
    fields = diffuse(diffuse(chemical_fractions, coeff), coeff)
    flat = fields.reshape(S, MESH_LEADING * MESH_TRAILING, STACK_HEIGHT)
    enthalpy_output = thermal_state.reshape(MESH_LEADING * MESH_TRAILING, STACK_HEIGHT)
    react_mat = incoming_stoichiometry.astype(jnp.float32)
    react_tr = react_mat.T
    prod_tr = outgoing_stoichiometry.astype(jnp.float32).T
    block_cols = 7 * BURN_MAX // 4
    total = N_WIDE * (N_NARROW // 4) * block_cols
    chosen = jnp.nonzero(ignited_stacks.reshape(-1), size=total)[0].astype(jnp.int32)
    blocks = chosen.reshape(-1, block_cols)

    def one_block(cols):
        picked = jnp.take(flat, cols, axis=1).reshape(S, -1)
        temps = jnp.take(enthalpy_output, cols, axis=0).reshape(-1)
        return react(picked, temps, natural_exponent_scale, arrhenius_energy, react_mat, react_tr, prod_tr).reshape(S, block_cols, STACK_HEIGHT)

    result = lax.map(one_block, blocks)
    result = jnp.transpose(result, (1, 0, 2, 3)).reshape(S, total, STACK_HEIGHT)
    flat = flat.at[:, chosen].set(result)
    return flat.reshape(S, MESH_LEADING, MESH_TRAILING, STACK_HEIGHT)
```

```python
import jax
import jax.numpy as jnp
from jax import lax
from jax.experimental import pallas as pl
from jax.experimental.pallas import tpu as pltpu
from jax.sharding import PartitionSpec as P

BURN_MAX = 8
S = 53
R = 325
SP = 64
RP = 328
H = 128


VM = pl.BlockSpec(memory_space=pltpu.VMEM)
SM = pl.BlockSpec(memory_space=pltpu.SMEM)


def pack_kernel(info, x, long_out, short_out, diag_out):
    w = info[0]
    p = info[1]
    long_near = jnp.where(p == 0, 0, 7)
    long_far = jnp.where(p == 0, 1, 6)
    short_near = 7 - long_near
    short_far = 7 - long_far
    for r in range(2):
        long_out[:, r : r + 1, :] = x[:, r, pl.ds(long_near, 1), :]
        long_out[:, 2 + r : 3 + r, :] = x[:, r, pl.ds(long_far, 1), :]
        short_out[:, r : r + 1, :] = x[:, r, pl.ds(short_near, 1), :]
        short_out[:, 2 + r : 3 + r, :] = x[:, r, pl.ds(short_far, 1), :]
    row = jnp.where(w == 0, 0, 1)
    diag_out[...] = x[:, row, pl.ds(long_near, 1), :]


def rows_kernel(info, x, short, up_out, down_out, wrap_out):
    w = info[0]
    p = info[1]
    edge = lax.broadcasted_iota(jnp.int32, (8, H), 0) == jnp.where(p == 0, 7, 0)
    first = jnp.where(w == 0, 1.0, 0.0)
    for s in range(S):
        v0 = x[s, 0]
        v1 = x[s, 1]
        f0 = jnp.where(edge, 2.0 * short[s, 1:2, :], 0.0)
        f1 = jnp.where(edge, 2.0 * short[s, 0:1, :], 0.0)
        up_out[s, 0] = v0 + f0
        up_out[s, 1] = v1
        down_out[s, 0] = v0
        down_out[s, 1] = v1 + f1
        wrap_out[s, 0] = v0 + f0 * (1.0 - first)
        wrap_out[s, 1] = v1 + f1 * first


def around(v):
    return pltpu.roll(v, 1, 1) + pltpu.roll(v, H - 1, 1)


def final_kernel(
    info,
    marks,
    spread,
    x,
    from_below,
    from_above,
    wrapped,
    short,
    long,
    corner_below,
    corner_above,
    corner_diag,
    temps,
    scale,
    energy,
    left,
    right,
    out,
    index,
    stack,
):
    w = info[0]
    p = info[1]
    last = info[2]
    even = p == 0
    at_first = w == 0
    at_last = w == last
    sub = lax.broadcasted_iota(jnp.int32, (8, H), 0)
    is_lo = sub == 0
    is_hi = sub == 7
    long_edge = sub == jnp.where(even, 0, 7)

    def beside(v, lo, hi):
        down = jnp.where(is_lo, lo, pltpu.roll(v, 1, 0))
        up = jnp.where(is_hi, hi, pltpu.roll(v, 7, 0))
        return down + up

    for s in range(S):
        c = spread[s]
        v0 = x[s, 0]
        v1 = x[s, 1]
        below_far = jnp.where(at_first, wrapped[s, 0], from_below[s, 0])
        below = jnp.where(at_first, wrapped[s, 1], from_below[s, 1])
        above = jnp.where(at_last, wrapped[s, 0], from_above[s, 0])
        above_far = jnp.where(at_last, wrapped[s, 1], from_above[s, 1])
        cb = jnp.where(at_first, corner_diag[s], corner_below[s])
        ca = jnp.where(at_last, corner_diag[s], corner_above[s])
        below_far = below_far + jnp.where(long_edge, 2.0 * cb, 0.0)
        above_far = above_far + jnp.where(long_edge, 2.0 * ca, 0.0)
        lo = jnp.where(even, long[s], short[s])
        hi = jnp.where(even, short[s], long[s])
        u_lo = []
        u_hi = []
        for r in range(2):
            v = (v0, v1)[r]
            for side, edge, got in ((lo, 0, u_lo), (hi, 7, u_hi)):
                near = side[r : r + 1]
                n = side[2 + r : 3 + r] + side[1 - r : 2 - r] + v[edge : edge + 1] + around(near)
                got.append(near + c * (n - 6.0 * near))
        u0 = v0 + c * (below + v1 + beside(v0, lo[0:1], hi[0:1]) + around(v0) - 6.0 * v0)
        u1 = v1 + c * (v0 + above + beside(v1, lo[1:2], hi[1:2]) + around(v1) - 6.0 * v1)
        ub = below + c * (below_far + v0 + beside(below, 0.0, 0.0) + around(below) - 6.0 * below)
        ua = above + c * (above_far + v1 + beside(above, 0.0, 0.0) + around(above) - 6.0 * above)
        m0 = u0 + c * (ub + u1 + beside(u0, u_lo[0], u_hi[0]) + around(u0) - 6.0 * u0)
        m1 = u1 + c * (u0 + ua + beside(u1, u_lo[1], u_hi[1]) + around(u1) - 6.0 * u1)
        out[16 * s : 16 * s + 8, :] = m0
        out[16 * s + 8 : 16 * s + 16, :] = m1

    count = 0
    for col in range(16):
        index[count] = col
        count = count + marks[col // 8, col % 8]

    stack[...] = jnp.zeros(stack.shape, jnp.bfloat16)

    def react(cols):
        n = cols * H
        where = [index[i] for i in range(cols)]
        v = jnp.concatenate([out[pl.ds(i, S, stride=16), :] for i in where], axis=1)
        inv = 1.0 / jnp.concatenate([temps[pl.ds(i, 1), :] for i in where], axis=1)
        base = scale[...] - energy[...] * inv
        for substep in range(2):
            logs = jnp.log(v)
            top = logs.astype(jnp.bfloat16)
            rest = logs - top.astype(jnp.float32)
            mid = rest.astype(jnp.bfloat16)
            low = (rest - mid.astype(jnp.float32)).astype(jnp.bfloat16)
            stack[0:S, :n] = top
            stack[SP : SP + S, :n] = mid
            stack[2 * SP : 2 * SP + S, :n] = low
            expo = base + jnp.dot(left[...], stack[:, :n], preferred_element_type=jnp.float32)
            rates = jnp.exp(expo)
            top = rates.astype(jnp.bfloat16)
            low = (rates - top.astype(jnp.float32)).astype(jnp.bfloat16)
            both = jnp.dot(right[...], top, preferred_element_type=jnp.float32)
            both = both + jnp.dot(right[...], low, preferred_element_type=jnp.float32)
            v = v * (v + 0.5 * both[0:S]) / (v + 0.5 * both[SP : SP + S])
        for k, i in enumerate(where):
            out[pl.ds(i, S, stride=16), :] = v[:, k * H : (k + 1) * H]

    few = BURN_MAX // 4

    @pl.when(count > few)
    def _():
        react(BURN_MAX)

    @pl.when(count <= few)
    def _():
        react(few)


def sds(*shape):
    return jax.ShapeDtypeStruct(shape, jnp.float32)


def shards(
    chemical_fractions,
    thermal_state,
    ignited_stacks,
    spreading_number,
    natural_exponent_scale,
    arrhenius_energy,
    incoming_stoichiometry,
    outgoing_stoichiometry,
):
    x = chemical_fractions
    nw = lax.axis_size("wide")
    nn = lax.axis_size("narrow")
    w = lax.axis_index("wide")
    n = lax.axis_index("narrow")
    info = jnp.stack([w, n % 2, jnp.int32(nw - 1)]).astype(jnp.int32)

    long_msg, short_msg, diag_msg = pl.pallas_call(
        pack_kernel,
        out_shape=(sds(S, 4, H), sds(S, 4, H), sds(S, 1, H)),
        in_specs=[SM, VM],
        out_specs=(VM, VM, VM),
        name="pack",
    )(info, x)

    near_pair = [(i, i ^ 1) for i in range(nn)]
    partner = [(i + 1) % nn if i % 2 else (i - 1) % nn for i in range(nn)]
    far_pair = [(i, partner[i]) for i in range(nn)]
    short = lax.ppermute(short_msg, "narrow", near_pair)
    long = lax.ppermute(long_msg, "narrow", far_pair)

    up_msg, down_msg, wrap_msg = pl.pallas_call(
        rows_kernel,
        out_shape=(sds(S, 2, 8, H),) * 3,
        in_specs=[SM, VM, VM],
        out_specs=(VM, VM, VM),
        name="rows",
    )(info, x, short)
    ends = [(0, nw - 1), (nw - 1, 0)]
    up = [(i, i + 1) for i in range(nw - 1)]
    down = [(i + 1, i) for i in range(nw - 1)]
    wrapped = lax.ppermute(wrap_msg, "wide", ends)
    from_below = lax.ppermute(up_msg, "wide", up)
    from_above = lax.ppermute(down_msg, "wide", down)
    across = [(a * nn + i, b * nn + partner[i]) for a, b in ends for i in range(nn)]
    corner_diag = lax.ppermute(diag_msg, ("wide", "narrow"), across)
    corner_below = lax.ppermute(long[:, 1:2], "wide", up)
    corner_above = lax.ppermute(long[:, 0:1], "wide", down)

    bf = jnp.bfloat16
    pad = ((0, RP - R), (0, SP - S))
    react_mat = jnp.pad(incoming_stoichiometry.astype(bf), pad)
    prod_mat = jnp.pad(outgoing_stoichiometry.astype(bf), pad)
    left = jnp.concatenate([react_mat] * 3, axis=1)
    right = jnp.concatenate([prod_mat, react_mat], axis=1).T
    scale = jnp.pad(natural_exponent_scale, (0, RP - R))[:, None]
    energy = jnp.pad(arrhenius_energy, (0, RP - R))[:, None]

    out = pl.pallas_call(
        final_kernel,
        out_shape=sds(S * 16, H),
        in_specs=[SM, SM, SM] + [VM] * 14,
        out_specs=VM,
        scratch_shapes=[pltpu.SMEM((17,), jnp.int32), pltpu.VMEM((3 * SP, BURN_MAX * H), bf)],
        name="step",
    )(
        info,
        ignited_stacks,
        spreading_number,
        x,
        from_below,
        from_above,
        wrapped,
        short,
        long,
        corner_below,
        corner_above,
        corner_diag,
        thermal_state.reshape(16, H),
        scale,
        energy,
        left,
        right,
    )
    return out.reshape(S, 2, 8, H)


def solution(mesh):
    in_specs = (
        P(None, "wide", "narrow", None),
        P("wide", "narrow", None),
        P("wide", "narrow"),
        P(),
        P(),
        P(),
        P(),
        P(),
    )
    out_specs = P(None, "wide", "narrow", None)
    return jax.shard_map(shards, mesh=mesh, in_specs=in_specs, out_specs=out_specs, check_vma=False)
```

```python
import jax
import jax.numpy as jnp
from jax import lax
from jax.experimental import pallas as pl
from jax.experimental.pallas import tpu as pltpu
from jax.sharding import PartitionSpec as P


BURN_MAX = 8
S = 53
R = 325
SP = 64
RP = 328
H = 128


VM = pl.BlockSpec(memory_space=pltpu.VMEM)
SM = pl.BlockSpec(memory_space=pltpu.SMEM)


def pack_kernel(x, long_out, short_out, up_out, down_out):
    p = lax.axis_index("narrow") % 2
    long_near = jnp.where(p == 0, 0, 7)
    long_far = jnp.where(p == 0, 1, 6)
    short_near = 7 - long_near
    short_far = 7 - long_far
    for r, row_out in ((0, down_out), (1, up_out)):
        long_edge = x[:, r, pl.ds(long_near, 1), :]
        short_edge = x[:, r, pl.ds(short_near, 1), :]
        long_out[:, r : r + 1, :] = long_edge
        short_out[:, r : r + 1, :] = short_edge
        row_out[:, 0:1, :] = long_edge
        row_out[:, 1:2, :] = short_edge
        long_out[:, 2 + r : 3 + r, :] = x[:, r, pl.ds(long_far, 1), :]
        short_out[:, 2 + r : 3 + r, :] = x[:, r, pl.ds(short_far, 1), :]


def fold_kernel(long, short, below, above, long_out, short_out):
    long_out[:, 0:2, :] = long[:, 0:2, :]
    short_out[:, 0:2, :] = short[:, 0:2, :]
    w = lax.axis_index("wide")
    low = jnp.where(w == 0, 0.0, 2.0)
    high = jnp.where(w == lax.axis_size("wide") - 1, 0.0, 2.0)
    long_out[:, 2:3, :] = long[:, 2:3, :] + low * below[:, 0:1, :]
    long_out[:, 3:4, :] = long[:, 3:4, :] + high * above[:, 0:1, :]
    short_out[:, 2:3, :] = short[:, 2:3, :] + low * below[:, 1:2, :]
    short_out[:, 3:4, :] = short[:, 3:4, :] + high * above[:, 1:2, :]


def first_edge_kernel(up, out):
    at = jnp.where(lax.axis_index("narrow") % 2 == 0, 7, 0)
    out[...] = up[:, 1, pl.ds(at, 1), :]


def edge_kernel(up, down, out):
    at = jnp.where(lax.axis_index("narrow") % 2 == 0, 7, 0)
    first = lax.axis_index("wide") == 0
    out[...] = jnp.where(first, up[:, 1, pl.ds(at, 1), :], down[:, 0, pl.ds(at, 1), :])


def around(v):
    return pltpu.roll(v, 1, 1) + pltpu.roll(v, H - 1, 1)


def final_kernel(
    marks,
    spread,
    x,
    up_0,
    up_1,
    down_0,
    down_1,
    short,
    long_d,
    long_b,
    long_c,
    diag_below,
    diag_above,
    across_a,
    across_b,
    corner_0,
    corner_1,
    temps,
    rate,
    left,
    right,
    out,
    index,
    stack,
):
    w = lax.axis_index("wide")
    p = lax.axis_index("narrow") % 2
    last = lax.axis_size("wide") - 1
    even = p == 0
    at_first = w == 0
    at_last = w == last
    sub = lax.broadcasted_iota(jnp.int32, (8, H), 0)
    is_lo = sub == 0
    is_hi = sub == 7
    long_edge = jnp.where(even, 0, 7)
    long_first = sub == jnp.where(at_first, long_edge, 8)
    long_last = sub == jnp.where(at_last, long_edge, 8)
    short_first = sub == jnp.where(at_first, 7 - long_edge, 8)
    short_last = sub == jnp.where(at_last, 7 - long_edge, 8)

    def beside(v, lo, hi):
        down = jnp.where(is_lo, lo, pltpu.roll(v, 1, 0))
        up = jnp.where(is_hi, hi, pltpu.roll(v, 7, 0))
        return down + up

    for s in range(S):
        c = spread[s]
        v0 = x[s, 0]
        v1 = x[s, 1]
        below_rows = up_0[s] + up_1[s]
        above_rows = down_0[s] + down_1[s]
        below_far = below_rows[0]
        below = below_rows[1]
        above = above_rows[0]
        above_far = above_rows[1]
        near_corner = 2.0 * (corner_0[s] + corner_1[s])
        below_far = below_far + jnp.where(long_first, 2.0 * (diag_below[s, 0:1, :] + across_a[s, 0:1, :]), 0.0)
        above_far = above_far + jnp.where(long_last, 2.0 * (diag_above[s, 0:1, :] + across_b[s, 0:1, :]), 0.0)
        below_far = below_far + jnp.where(short_first, near_corner, 0.0)
        above_far = above_far + jnp.where(short_last, near_corner, 0.0)
        long_s = long_d[s] + long_b[s] + long_c[s]
        lo = jnp.where(even, long_s, short[s])
        hi = jnp.where(even, short[s], long_s)
        u_lo = []
        u_hi = []
        for r in range(2):
            v = (v0, v1)[r]
            for side, edge, got in ((lo, 0, u_lo), (hi, 7, u_hi)):
                near = side[r : r + 1]
                n = side[2 + r : 3 + r] + side[1 - r : 2 - r] + v[edge : edge + 1] + around(near)
                got.append(near + c * (n - 6.0 * near))
        u0 = v0 + c * (below + v1 + beside(v0, lo[0:1], hi[0:1]) + around(v0) - 6.0 * v0)
        u1 = v1 + c * (v0 + above + beside(v1, lo[1:2], hi[1:2]) + around(v1) - 6.0 * v1)
        ub = below + c * (below_far + v0 + beside(below, 0.0, 0.0) + around(below) - 6.0 * below)
        ua = above + c * (above_far + v1 + beside(above, 0.0, 0.0) + around(above) - 6.0 * above)
        m0 = u0 + c * (ub + u1 + beside(u0, u_lo[0], u_hi[0]) + around(u0) - 6.0 * u0)
        m1 = u1 + c * (u0 + ua + beside(u1, u_lo[1], u_hi[1]) + around(u1) - 6.0 * u1)
        out[16 * s : 16 * s + 8, :] = m0
        out[16 * s + 8 : 16 * s + 16, :] = m1

    count = 0
    for col in range(16):
        index[count] = col
        count = count + marks[col // 8, col % 8]

    stack[...] = jnp.zeros(stack.shape, jnp.bfloat16)

    def react(cols):
        n = cols * H
        where = [index[i] for i in range(cols)]
        v = jnp.concatenate([out[pl.ds(i, S, stride=16), :] for i in where], axis=1)
        inv = 1.0 / jnp.concatenate([temps[pl.ds(i, 1), :] for i in where], axis=1)
        base = rate[:, 0:1] - rate[:, 1:2] * inv
        for _ in range(2):
            logs = jnp.log(v)
            top = logs.astype(jnp.bfloat16)
            rest = logs - top.astype(jnp.float32)
            mid = rest.astype(jnp.bfloat16)
            low = (rest - mid.astype(jnp.float32)).astype(jnp.bfloat16)
            stack[0:S, :n] = top
            stack[SP : SP + S, :n] = mid
            stack[2 * SP : 2 * SP + S, :n] = low
            expo = base + jnp.dot(left[...], stack[:, :n], preferred_element_type=jnp.float32)
            rates = jnp.exp(expo)
            top = rates.astype(jnp.bfloat16)
            low = (rates - top.astype(jnp.float32)).astype(jnp.bfloat16)
            both = jnp.dot(right[...], top, preferred_element_type=jnp.float32)
            both = both + jnp.dot(right[...], low, preferred_element_type=jnp.float32)
            v = v * (v + 0.5 * both[0:S]) / (v + 0.5 * both[SP : SP + S])
        for k, i in enumerate(where):
            out[pl.ds(i, S, stride=16), :] = v[:, k * H : (k + 1) * H]

    few = BURN_MAX // 4

    @pl.when(count > few)
    def _():
        react(BURN_MAX)

    @pl.when(count <= few)
    def _():
        react(few)


def sds(*shape):
    return jax.ShapeDtypeStruct(shape, jnp.float32)


def vds(*shape):
    return pltpu.VMEM(shape, jnp.float32)


def vmem(value):
    return pltpu.with_memory_space_constraint(value, pltpu.VMEM)


def shards(
    chemical_fractions,
    thermal_state,
    ignited_stacks,
    spreading_number,
    natural_exponent_scale,
    arrhenius_energy,
    incoming_stoichiometry,
    outgoing_stoichiometry,
):
    x = chemical_fractions
    nw = lax.axis_size("wide")
    nn = lax.axis_size("narrow")
    up = [(i, i + 1) for i in range(nw - 1)]
    down = [(i + 1, i) for i in range(nw - 1)]
    partner = [(i + 1) % nn if i % 2 else (i - 1) % nn for i in range(nn)]
    both = ("wide", "narrow")
    end = nw - 1
    half = nw // 2
    early = [i for i in range(nn) if i // 2 % 2 == 0]
    late = [i for i in range(nn) if i // 2 % 2 == 1]

    def at(i, j):
        return i * nn + j

    bf = jnp.bfloat16
    pad = ((0, RP - R), (0, SP - S))
    react_mat = jnp.pad(incoming_stoichiometry.astype(bf), pad)
    prod_mat = jnp.pad(outgoing_stoichiometry.astype(bf), pad)
    left = jnp.concatenate([react_mat] * 3, axis=1)
    right = jnp.concatenate([prod_mat, react_mat], axis=1).T
    rate = jnp.stack([natural_exponent_scale, arrhenius_energy], axis=1)
    rate = jnp.pad(rate, ((0, RP - R), (0, 0)))

    first_half = [(i, j) for i in range(half - 1) for j in early]
    others = [(i, j) for i in range(end) for j in range(nn) if i >= half - 1 or j in late]
    up_0 = lax.ppermute(
        x,
        both,
        [(at(i, j), at(i + 1, j)) for i, j in first_half]
        + [(at(end, j), at(0, j)) for j in early],
    )
    down_0 = lax.ppermute(x, both, [(at(i + 1, j), at(i, j)) for i, j in first_half])
    long_raw, short_raw, up_msg, down_msg = pl.pallas_call(
        pack_kernel,
        out_shape=(vds(S, 4, H), vds(S, 4, H), vds(S, 2, H), vds(S, 2, H)),
        in_specs=[VM],
        out_specs=(VM,) * 4,
        name="pack",
    )(x)
    corner_below = lax.ppermute(
        up_msg,
        both,
        [(at(a, j), at(b, j)) for a, b in up for j in range(nn)]
        + [(at(end, partner[j]), at(0, j)) for j in late],
    )
    corner_above = lax.ppermute(
        down_msg,
        both,
        [(at(a, j), at(b, j)) for a, b in down for j in range(nn)]
        + [(at(0, j), at(end, partner[j])) for j in late],
    )
    across_a = lax.ppermute(up_msg, both, [(at(end, partner[j]), at(0, j)) for j in early])
    across_b = lax.ppermute(down_msg, both, [(at(0, j), at(end, partner[j])) for j in early])
    long_msg, short_msg = pl.pallas_call(
        fold_kernel,
        out_shape=(vds(S, 4, H), vds(S, 4, H)),
        in_specs=[VM] * 4,
        out_specs=(VM,) * 2,
        name="fold",
    )(vmem(long_raw), vmem(short_raw), vmem(corner_below), vmem(corner_above))

    def long_swap(senders):
        return lax.ppermute(long_msg, both, [(at(i, j), at(i, partner[j])) for i, j in senders])

    long_b = long_swap([(i, j) for i in range(end) for j in range(nn) if i or j in late])
    up_1 = lax.ppermute(
        x,
        both,
        [(at(i, j), at(i + 1, j)) for i, j in others] + [(at(end, j), at(0, j)) for j in late],
    )
    down_1 = lax.ppermute(
        x,
        both,
        [(at(i + 1, j), at(i, j)) for i, j in others]
        + [(at(0, j), at(end, j)) for j in range(nn)],
    )
    short_msg, left, right, rate = lax.optimization_barrier((short_msg, left, right, rate))
    short = lax.ppermute(short_msg, "narrow", [(j, j ^ 1) for j in range(nn)])
    long_c = long_swap([(0, j) for j in early])
    long_d = long_swap([(end, j) for j in range(nn)])
    edge_0 = pl.pallas_call(
        first_edge_kernel,
        out_shape=vds(S, 1, H),
        in_specs=[VM],
        out_specs=VM,
        name="edge_0",
    )(vmem(up_0))
    corner_0 = lax.ppermute(edge_0, both, [(at(0, j), at(0, j ^ 1)) for j in early])
    edge_1 = pl.pallas_call(
        edge_kernel,
        out_shape=vds(S, 1, H),
        in_specs=[VM] * 2,
        out_specs=VM,
        name="edge_1",
    )(vmem(up_1), vmem(down_1))
    corner_1 = lax.ppermute(
        edge_1,
        both,
        [(at(0, j), at(0, j ^ 1)) for j in late] + [(at(end, j), at(end, j ^ 1)) for j in range(nn)],
    )

    out = pl.pallas_call(
        final_kernel,
        out_shape=sds(S * 16, H),
        in_specs=[SM, SM] + [VM] * 19,
        out_specs=VM,
        scratch_shapes=[pltpu.SMEM((17,), jnp.int32), pltpu.VMEM((3 * SP, BURN_MAX * H), bf)],
        name="step",
    )(
        ignited_stacks,
        spreading_number,
        x,
        vmem(up_0),
        vmem(up_1),
        vmem(down_0),
        vmem(down_1),
        vmem(short),
        vmem(long_d),
        vmem(long_b),
        vmem(long_c),
        vmem(corner_below),
        vmem(corner_above),
        vmem(across_a),
        vmem(across_b),
        vmem(corner_0),
        vmem(corner_1),
        thermal_state.reshape(16, H),
        rate,
        left,
        right,
    )
    return out.reshape(S, 2, 8, H)


def solution(mesh):
    in_specs = (
        P(None, "wide", "narrow", None),
        P("wide", "narrow", None),
        P("wide", "narrow"),
        P(),
        P(),
        P(),
        P(),
        P(),
    )
    out_specs = P(None, "wide", "narrow", None)
    return jax.shard_map(shards, mesh=mesh, in_specs=in_specs, out_specs=out_specs, check_vma=False)
```

```python
import jax
import jax.numpy as jnp
from jax import lax
from jax.experimental import pallas as pl
from jax.experimental.pallas import tpu as pltpu
from jax.sharding import PartitionSpec as P


BURN_MAX = 8
S = 53
R = 325
SP = 64
RP = 328
H = 128


VM = pl.BlockSpec(memory_space=pltpu.VMEM)
SM = pl.BlockSpec(memory_space=pltpu.SMEM)


def column(ref, row, col):
    return ref[pl.ds(8 * row + col, S, stride=16), :]


def pack_kernel(x, long_out, short_out, up_out, down_out):
    p = lax.axis_index("narrow") % 2
    long_near = jnp.where(p == 0, 0, 7)
    long_far = jnp.where(p == 0, 1, 6)
    for r, row_out in ((0, down_out), (1, up_out)):
        long_edge = column(x, r, long_near)
        short_edge = column(x, r, 7 - long_near)
        long_out[r] = long_edge
        short_out[r] = short_edge
        row_out[0] = long_edge
        row_out[1] = short_edge
        long_out[2 + r] = column(x, r, long_far)
        short_out[2 + r] = column(x, r, 7 - long_far)


def fold_kernel(long, short, below, above, long_out, short_out):
    w = lax.axis_index("wide")
    low = jnp.where(w == 0, 0.0, 2.0)
    high = jnp.where(w == lax.axis_size("wide") - 1, 0.0, 2.0)
    for k, got, out in ((0, long, long_out), (1, short, short_out)):
        out[0:2] = got[0:2]
        out[2] = got[2] + low * below[k]
        out[3] = got[3] + high * above[k]


def first_edge_kernel(up, out):
    at = jnp.where(lax.axis_index("narrow") % 2 == 0, 7, 0)
    out[...] = column(up, 1, at)


def edge_kernel(up, down, out):
    at = jnp.where(lax.axis_index("narrow") % 2 == 0, 7, 0)
    first = lax.axis_index("wide") == 0
    out[...] = jnp.where(first, column(up, 1, at), column(down, 0, at))


def around(v):
    return pltpu.roll(v, 1, 1) + pltpu.roll(v, H - 1, 1)


def final_kernel(
    marks,
    spread,
    x,
    up_0,
    up_1,
    down_0,
    down_1,
    short,
    long_d,
    long_b,
    long_c,
    diag_below,
    diag_above,
    across_a,
    across_b,
    corner_0,
    corner_1,
    temps,
    spread_column,
    rate,
    left,
    right,
    out,
    index,
    stack,
):
    w = lax.axis_index("wide")
    p = lax.axis_index("narrow") % 2
    last = lax.axis_size("wide") - 1
    even = p == 0
    at_first = w == 0
    at_last = w == last
    sub = lax.broadcasted_iota(jnp.int32, (8, H), 0)
    is_lo = sub == 0
    is_hi = sub == 7

    def beside(v):
        down = jnp.where(is_lo, 0.0, pltpu.roll(v, 1, 0))
        up = jnp.where(is_hi, 0.0, pltpu.roll(v, 7, 0))
        return down + up

    for s in range(S):
        c = spread[s]
        keep = 1.0 - 6.0 * c
        at = 16 * s
        v0 = x[at : at + 8, :]
        v1 = x[at + 8 : at + 16, :]
        below_far = up_0[s, 0] + up_1[s, 0]
        below = up_0[s, 1] + up_1[s, 1]
        above = down_0[s, 0] + down_1[s, 0]
        above_far = down_0[s, 1] + down_1[s, 1]
        u0 = keep * v0 + c * (below + v1 + beside(v0) + around(v0))
        u1 = keep * v1 + c * (v0 + above + beside(v1) + around(v1))
        t0 = u0 + c * below
        t1 = u1 + c * above
        n0 = keep * below + c * (below_far + v0) + u1 + beside(t0) + around(t0)
        n1 = keep * above + c * (above_far + v1) + u0 + beside(t1) + around(t1)
        out[at : at + 8, :] = keep * u0 + c * n0
        out[at + 8 : at + 16, :] = keep * u1 + c * n1

    c = spread_column[...]
    c2 = c * c
    once = 2.0 * c * (1.0 - 6.0 * c)
    long_edge = jnp.where(even, 0, 7)
    low = jnp.where(at_first, 2.0, 0.0)
    high = jnp.where(at_last, 2.0, 0.0)
    long = [long_d[k] + long_b[k] + long_c[k] for k in range(4)]
    ends_long = (low * (diag_below[0] + across_a[0]), high * (diag_above[0] + across_b[0]))
    near_corner = corner_0[...] + corner_1[...]
    ends_short = (low * near_corner, high * near_corner)
    for got, ends, edge in (
        (long, ends_long, long_edge),
        ([short[k] for k in range(4)], ends_short, 7 - long_edge),
    ):
        inner = jnp.where(edge == 0, 1, 6)
        for r in range(2):
            near = got[r]
            add = once * near + c2 * (
                2.0 * (around(near) + got[1 - r]) + got[2 + r] + ends[r] + column(x, r, edge)
            )
            spot = pl.ds(8 * r + edge, S, stride=16)
            out[spot, :] = out[spot, :] + add
            spot = pl.ds(8 * r + inner, S, stride=16)
            out[spot, :] = out[spot, :] + c2 * near

    count = 0
    for col in range(16):
        index[count] = col
        count = count + marks[col // 8, col % 8]

    stack[...] = jnp.zeros(stack.shape, jnp.bfloat16)

    def react(cols):
        n = cols * H
        where = [index[i] for i in range(cols)]
        v = jnp.concatenate([out[pl.ds(i, S, stride=16), :] for i in where], axis=1)
        inv = 1.0 / jnp.concatenate([temps[pl.ds(i, 1), :] for i in where], axis=1)
        base = rate[:, 0:1] - rate[:, 1:2] * inv
        for _ in range(2):
            logs = jnp.log(v)
            top = logs.astype(jnp.bfloat16)
            rest = logs - top.astype(jnp.float32)
            mid = rest.astype(jnp.bfloat16)
            low = (rest - mid.astype(jnp.float32)).astype(jnp.bfloat16)
            stack[0:S, :n] = top
            stack[SP : SP + S, :n] = mid
            stack[2 * SP : 2 * SP + S, :n] = low
            expo = base + jnp.dot(left[...], stack[:, :n], preferred_element_type=jnp.float32)
            rates = jnp.exp(expo)
            top = rates.astype(jnp.bfloat16)
            low = (rates - top.astype(jnp.float32)).astype(jnp.bfloat16)
            both = jnp.dot(right[...], top, preferred_element_type=jnp.float32)
            both = both + jnp.dot(right[...], low, preferred_element_type=jnp.float32)
            v = v * (v + 0.5 * both[0:S]) / (v + 0.5 * both[SP : SP + S])
        for k, i in enumerate(where):
            out[pl.ds(i, S, stride=16), :] = v[:, k * H : (k + 1) * H]

    few = BURN_MAX // 4

    @pl.when(count > few)
    def _():
        react(BURN_MAX)

    @pl.when(count <= few)
    def _():
        react(few)


def sds(*shape):
    return jax.ShapeDtypeStruct(shape, jnp.float32)


def vds(*shape):
    return pltpu.VMEM(shape, jnp.float32)


def vmem(value):
    return pltpu.with_memory_space_constraint(value, pltpu.VMEM)


def shards(
    chemical_fractions,
    thermal_state,
    ignited_stacks,
    spreading_number,
    natural_exponent_scale,
    arrhenius_energy,
    incoming_stoichiometry,
    outgoing_stoichiometry,
):
    x = chemical_fractions
    nw = lax.axis_size("wide")
    nn = lax.axis_size("narrow")
    up = [(i, i + 1) for i in range(nw - 1)]
    down = [(i + 1, i) for i in range(nw - 1)]
    partner = [(i + 1) % nn if i % 2 else (i - 1) % nn for i in range(nn)]
    both = ("wide", "narrow")
    end = nw - 1
    half = nw // 2
    early = [i for i in range(nn) if i // 2 % 2 == 0]
    late = [i for i in range(nn) if i // 2 % 2 == 1]

    def at(i, j):
        return i * nn + j

    bf = jnp.bfloat16
    pad = ((0, RP - R), (0, SP - S))
    react_mat = jnp.pad(incoming_stoichiometry.astype(bf), pad)
    prod_mat = jnp.pad(outgoing_stoichiometry.astype(bf), pad)
    left = jnp.concatenate([react_mat] * 3, axis=1)
    right = jnp.concatenate([prod_mat, react_mat], axis=1).T
    rate = jnp.stack([natural_exponent_scale, arrhenius_energy], axis=1)
    rate = jnp.pad(rate, ((0, RP - R), (0, 0)))

    first_half = [(i, j) for i in range(half - 1) for j in early]
    others = [(i, j) for i in range(end) for j in range(nn) if i >= half - 1 or j in late]
    up_0 = lax.ppermute(
        x,
        both,
        [(at(i, j), at(i + 1, j)) for i, j in first_half]
        + [(at(end, j), at(0, j)) for j in early],
    )
    down_0 = lax.ppermute(x, both, [(at(i + 1, j), at(i, j)) for i, j in first_half])
    long_raw, short_raw, up_msg, down_msg = pl.pallas_call(
        pack_kernel,
        out_shape=(vds(4, S, H), vds(4, S, H), vds(2, S, H), vds(2, S, H)),
        in_specs=[VM],
        out_specs=(VM,) * 4,
        name="pack",
    )(x.reshape(S * 16, H))
    corner_below = lax.ppermute(
        up_msg,
        both,
        [(at(a, j), at(b, j)) for a, b in up for j in range(nn)]
        + [(at(end, partner[j]), at(0, j)) for j in late],
    )
    corner_above = lax.ppermute(
        down_msg,
        both,
        [(at(a, j), at(b, j)) for a, b in down for j in range(nn)]
        + [(at(0, j), at(end, partner[j])) for j in late],
    )
    across_a = lax.ppermute(up_msg, both, [(at(end, partner[j]), at(0, j)) for j in early])
    across_b = lax.ppermute(down_msg, both, [(at(0, j), at(end, partner[j])) for j in early])
    long_msg, short_msg = pl.pallas_call(
        fold_kernel,
        out_shape=(vds(4, S, H), vds(4, S, H)),
        in_specs=[VM] * 4,
        out_specs=(VM,) * 2,
        name="fold",
    )(vmem(long_raw), vmem(short_raw), vmem(corner_below), vmem(corner_above))

    def long_swap(senders):
        return lax.ppermute(long_msg, both, [(at(i, j), at(i, partner[j])) for i, j in senders])

    long_b = long_swap([(i, j) for i in range(end) for j in range(nn) if i or j in late])
    up_1 = lax.ppermute(
        x,
        both,
        [(at(i, j), at(i + 1, j)) for i, j in others] + [(at(end, j), at(0, j)) for j in late],
    )
    down_1 = lax.ppermute(
        x,
        both,
        [(at(i + 1, j), at(i, j)) for i, j in others]
        + [(at(0, j), at(end, j)) for j in range(nn)],
    )
    spread_column = spreading_number[:, None]
    short_msg, left, right, rate, spread_column = lax.optimization_barrier(
        (short_msg, left, right, rate, spread_column)
    )
    short = lax.ppermute(short_msg, "narrow", [(j, j ^ 1) for j in range(nn)])
    long_c = long_swap([(0, j) for j in early])
    long_d = long_swap([(end, j) for j in range(nn)])
    edge_0 = pl.pallas_call(
        first_edge_kernel,
        out_shape=vds(S, H),
        in_specs=[VM],
        out_specs=VM,
        name="edge_0",
    )(vmem(up_0.reshape(S * 16, H)))
    corner_0 = lax.ppermute(edge_0, both, [(at(0, j), at(0, j ^ 1)) for j in early])
    edge_1 = pl.pallas_call(
        edge_kernel,
        out_shape=vds(S, H),
        in_specs=[VM] * 2,
        out_specs=VM,
        name="edge_1",
    )(vmem(up_1.reshape(S * 16, H)), vmem(down_1.reshape(S * 16, H)))
    corner_1 = lax.ppermute(
        edge_1,
        both,
        [(at(0, j), at(0, j ^ 1)) for j in late] + [(at(end, j), at(end, j ^ 1)) for j in range(nn)],
    )

    out = pl.pallas_call(
        final_kernel,
        out_shape=sds(S * 16, H),
        in_specs=[SM, SM] + [VM] * 20,
        out_specs=VM,
        scratch_shapes=[pltpu.SMEM((17,), jnp.int32), pltpu.VMEM((3 * SP, BURN_MAX * H), bf)],
        name="step",
    )(
        ignited_stacks,
        spreading_number,
        x.reshape(S * 16, H),
        vmem(up_0),
        vmem(up_1),
        vmem(down_0),
        vmem(down_1),
        vmem(short),
        vmem(long_d),
        vmem(long_b),
        vmem(long_c),
        vmem(corner_below),
        vmem(corner_above),
        vmem(across_a),
        vmem(across_b),
        vmem(corner_0),
        vmem(corner_1),
        thermal_state.reshape(16, H),
        spread_column,
        rate,
        left,
        right,
    )
    return out.reshape(S, 2, 8, H)


def solution(mesh):
    in_specs = (
        P(None, "wide", "narrow", None),
        P("wide", "narrow", None),
        P("wide", "narrow"),
        P(),
        P(),
        P(),
        P(),
        P(),
    )
    out_specs = P(None, "wide", "narrow", None)
    return jax.shard_map(shards, mesh=mesh, in_specs=in_specs, out_specs=out_specs, check_vma=False)
```

```python
import jax
import jax.numpy as jnp
from jax import lax
from jax.experimental import pallas as pl
from jax.experimental.pallas import tpu as pltpu
from jax.sharding import PartitionSpec as P


BURN_MAX = 8
S = 53
R = 325
SP = 64
RP = 328
H = 128


VM = pl.BlockSpec(memory_space=pltpu.VMEM)
SM = pl.BlockSpec(memory_space=pltpu.SMEM)


def column(ref, row, col):
    return ref[pl.ds(8 * row + col, S, stride=16), :]


def pack_kernel(x, long_out, short_out, up_out, down_out):
    p = lax.axis_index("narrow") % 2
    long_near = jnp.where(p == 0, 0, 7)
    long_far = jnp.where(p == 0, 1, 6)
    for r, row_out in ((0, down_out), (1, up_out)):
        long_edge = column(x, r, long_near)
        short_edge = column(x, r, 7 - long_near)
        long_out[r] = long_edge
        short_out[r] = short_edge
        row_out[0] = long_edge
        row_out[1] = short_edge
        long_out[2 + r] = column(x, r, long_far)
        short_out[2 + r] = column(x, r, 7 - long_far)


def fold_kernel(long, short, below, above, long_out, short_out):
    w = lax.axis_index("wide")
    low = jnp.where(w == 0, 0.0, 2.0)
    high = jnp.where(w == lax.axis_size("wide") - 1, 0.0, 2.0)
    for k, got, out in ((0, long, long_out), (1, short, short_out)):
        out[0:2] = got[0:2]
        out[2] = got[2] + low * below[k]
        out[3] = got[3] + high * above[k]


def first_edge_kernel(up, out):
    at = jnp.where(lax.axis_index("narrow") % 2 == 0, 7, 0)
    out[...] = column(up, 1, at)


def edge_kernel(up, down, out):
    at = jnp.where(lax.axis_index("narrow") % 2 == 0, 7, 0)
    first = lax.axis_index("wide") == 0
    out[...] = jnp.where(first, column(up, 1, at), column(down, 0, at))


def hold_kernel(left, right, rate, left_out, right_out, rate_out):
    left_out[...] = left[...]
    right_out[...] = right[...]
    rate_out[...] = rate[...]


def around(v):
    return pltpu.roll(v, 1, 1) + pltpu.roll(v, H - 1, 1)


def final_kernel(
    marks,
    spread,
    x,
    up_0,
    up_1,
    down_0,
    down_1,
    short,
    long_d,
    long_b,
    long_c,
    diag_below,
    diag_above,
    across_a,
    across_b,
    corner_0,
    corner_1,
    temps,
    rate,
    left,
    right,
    out,
    index,
    stack,
    spread_column,
):
    w = lax.axis_index("wide")
    p = lax.axis_index("narrow") % 2
    last = lax.axis_size("wide") - 1
    even = p == 0
    at_first = w == 0
    at_last = w == last
    sub = lax.broadcasted_iota(jnp.int32, (8, H), 0)
    is_lo = sub == 0
    is_hi = sub == 7

    def beside(v):
        down = jnp.where(is_lo, 0.0, pltpu.roll(v, 1, 0))
        up = jnp.where(is_hi, 0.0, pltpu.roll(v, 7, 0))
        return down + up

    for s in range(S):
        c = spread[s]
        keep = 1.0 - 6.0 * c
        spread_column[s : s + 1, :] = jnp.full((1, H), c)
        at = 16 * s
        v0 = x[at : at + 8, :]
        v1 = x[at + 8 : at + 16, :]
        far = pl.ds(at, 8)
        near = pl.ds(at + 8, 8)
        below_far = up_0[far, :] + up_1[far, :]
        below = up_0[near, :] + up_1[near, :]
        above = down_0[far, :] + down_1[far, :]
        above_far = down_0[near, :] + down_1[near, :]
        u0 = keep * v0 + c * (below + v1 + beside(v0) + around(v0))
        u1 = keep * v1 + c * (v0 + above + beside(v1) + around(v1))
        t0 = u0 + c * below
        t1 = u1 + c * above
        n0 = keep * below + c * (below_far + v0) + u1 + beside(t0) + around(t0)
        n1 = keep * above + c * (above_far + v1) + u0 + beside(t1) + around(t1)
        out[at : at + 8, :] = keep * u0 + c * n0
        out[at + 8 : at + 16, :] = keep * u1 + c * n1

    c = spread_column[...]
    c2 = c * c
    once = 2.0 * c * (1.0 - 6.0 * c)
    long_edge = jnp.where(even, 0, 7)
    low = jnp.where(at_first, 2.0, 0.0)
    high = jnp.where(at_last, 2.0, 0.0)
    long = [long_d[k] + long_b[k] + long_c[k] for k in range(4)]
    ends_long = (low * (diag_below[0] + across_a[0]), high * (diag_above[0] + across_b[0]))
    near_corner = corner_0[...] + corner_1[...]
    ends_short = (low * near_corner, high * near_corner)
    for got, ends, edge in (
        (long, ends_long, long_edge),
        ([short[k] for k in range(4)], ends_short, 7 - long_edge),
    ):
        inner = jnp.where(edge == 0, 1, 6)
        for r in range(2):
            near = got[r]
            add = once * near + c2 * (
                2.0 * (around(near) + got[1 - r]) + got[2 + r] + ends[r] + column(x, r, edge)
            )
            spot = pl.ds(8 * r + edge, S, stride=16)
            out[spot, :] = out[spot, :] + add
            spot = pl.ds(8 * r + inner, S, stride=16)
            out[spot, :] = out[spot, :] + c2 * near

    count = 0
    for col in range(16):
        index[count] = col
        count = count + marks[col // 8, col % 8]

    stack[...] = jnp.zeros(stack.shape, jnp.bfloat16)

    def react(cols):
        n = cols * H
        where = [index[i] for i in range(cols)]
        v = jnp.concatenate([out[pl.ds(i, S, stride=16), :] for i in where], axis=1)
        inv = 1.0 / jnp.concatenate([temps[pl.ds(i, 1), :] for i in where], axis=1)
        base = rate[:, 0:1] - rate[:, 1:2] * inv
        for _ in range(2):
            logs = jnp.log(v)
            top = logs.astype(jnp.bfloat16)
            rest = logs - top.astype(jnp.float32)
            mid = rest.astype(jnp.bfloat16)
            low = (rest - mid.astype(jnp.float32)).astype(jnp.bfloat16)
            stack[0:S, :n] = top
            stack[SP : SP + S, :n] = mid
            stack[2 * SP : 2 * SP + S, :n] = low
            expo = base + jnp.dot(left[...], stack[:, :n], preferred_element_type=jnp.float32)
            rates = jnp.exp(expo)
            top = rates.astype(jnp.bfloat16)
            low = (rates - top.astype(jnp.float32)).astype(jnp.bfloat16)
            both = jnp.dot(right[...], top, preferred_element_type=jnp.float32)
            both = both + jnp.dot(right[...], low, preferred_element_type=jnp.float32)
            v = v * (v + 0.5 * both[0:S]) / (v + 0.5 * both[SP : SP + S])
        for k, i in enumerate(where):
            out[pl.ds(i, S, stride=16), :] = v[:, k * H : (k + 1) * H]

    few = BURN_MAX // 4

    @pl.when(count > few)
    def _():
        react(BURN_MAX)

    @pl.when(count <= few)
    def _():
        react(few)


def sds(*shape):
    return jax.ShapeDtypeStruct(shape, jnp.float32)


def vds(*shape):
    return pltpu.VMEM(shape, jnp.float32)


def vmem(value):
    return pltpu.with_memory_space_constraint(value, pltpu.VMEM)


def shards(
    chemical_fractions,
    thermal_state,
    ignited_stacks,
    spreading_number,
    natural_exponent_scale,
    arrhenius_energy,
    incoming_stoichiometry,
    outgoing_stoichiometry,
):
    x = chemical_fractions
    nw = lax.axis_size("wide")
    nn = lax.axis_size("narrow")
    up = [(i, i + 1) for i in range(nw - 1)]
    down = [(i + 1, i) for i in range(nw - 1)]
    partner = [(i + 1) % nn if i % 2 else (i - 1) % nn for i in range(nn)]
    both = ("wide", "narrow")
    end = nw - 1
    half = nw // 2
    early = [i for i in range(nn) if i // 2 % 2 == 0]
    late = [i for i in range(nn) if i // 2 % 2 == 1]

    def at(i, j):
        return i * nn + j

    bf = jnp.bfloat16
    pad = ((0, RP - R), (0, SP - S))
    react_mat = jnp.pad(incoming_stoichiometry.astype(bf), pad)
    prod_mat = jnp.pad(outgoing_stoichiometry.astype(bf), pad)
    left = jnp.concatenate([react_mat] * 3, axis=1)
    right = jnp.concatenate([prod_mat, react_mat], axis=1).T
    rate = jnp.stack([natural_exponent_scale, arrhenius_energy], axis=1)
    rate = jnp.pad(rate, ((0, RP - R), (0, 0)))

    first_half = [(i, j) for i in range(half - 1) for j in early]
    others = [(i, j) for i in range(end) for j in range(nn) if i >= half - 1 or j in late]
    up_0 = lax.ppermute(
        x,
        both,
        [(at(i, j), at(i + 1, j)) for i, j in first_half]
        + [(at(end, j), at(0, j)) for j in early],
    )
    down_0 = lax.ppermute(x, both, [(at(i + 1, j), at(i, j)) for i, j in first_half])
    long_raw, short_raw, up_msg, down_msg = pl.pallas_call(
        pack_kernel,
        out_shape=(vds(4, S, H), vds(4, S, H), vds(2, S, H), vds(2, S, H)),
        in_specs=[VM],
        out_specs=(VM,) * 4,
        name="pack",
    )(x.reshape(S * 16, H))
    corner_below = lax.ppermute(
        up_msg,
        both,
        [(at(a, j), at(b, j)) for a, b in up for j in range(nn)]
        + [(at(end, partner[j]), at(0, j)) for j in late],
    )
    corner_above = lax.ppermute(
        down_msg,
        both,
        [(at(a, j), at(b, j)) for a, b in down for j in range(nn)]
        + [(at(0, j), at(end, partner[j])) for j in late],
    )
    across_a = lax.ppermute(up_msg, both, [(at(end, partner[j]), at(0, j)) for j in early])
    across_b = lax.ppermute(down_msg, both, [(at(0, j), at(end, partner[j])) for j in early])
    long_msg, short_msg = pl.pallas_call(
        fold_kernel,
        out_shape=(vds(4, S, H), vds(4, S, H)),
        in_specs=[VM] * 4,
        out_specs=(VM,) * 2,
        name="fold",
    )(vmem(long_raw), vmem(short_raw), vmem(corner_below), vmem(corner_above))

    def long_swap(senders):
        return lax.ppermute(long_msg, both, [(at(i, j), at(i, partner[j])) for i, j in senders])

    long_b = long_swap([(i, j) for i in range(end) for j in range(nn) if i or j in late])
    up_1 = lax.ppermute(
        x,
        both,
        [(at(i, j), at(i + 1, j)) for i, j in others] + [(at(end, j), at(0, j)) for j in late],
    )
    down_1 = lax.ppermute(
        x,
        both,
        [(at(i + 1, j), at(i, j)) for i, j in others]
        + [(at(0, j), at(end, j)) for j in range(nn)],
    )
    left, right, rate = pl.pallas_call(
        hold_kernel,
        out_shape=(
            jax.ShapeDtypeStruct(left.shape, bf),
            jax.ShapeDtypeStruct(right.shape, bf),
            jax.ShapeDtypeStruct(rate.shape, jnp.float32),
        ),
        in_specs=[VM] * 3,
        out_specs=(VM,) * 3,
        name="hold",
    )(left, right, rate)
    short_msg, left, right, rate = lax.optimization_barrier((short_msg, left, right, rate))
    short = lax.ppermute(short_msg, "narrow", [(j, j ^ 1) for j in range(nn)])
    long_c = long_swap([(0, j) for j in early])
    long_d = long_swap([(end, j) for j in range(nn)])
    rows = {id(v): v.reshape(S * 16, H) for v in (up_0, down_0)}
    rows |= {id(v): vmem(v.reshape(S * 16, H)) for v in (up_1, down_1)}

    def flat(value):
        return rows[id(value)]

    edge_0 = pl.pallas_call(
        first_edge_kernel,
        out_shape=vds(S, H),
        in_specs=[VM],
        out_specs=VM,
        name="edge_0",
    )(flat(up_0))
    corner_0 = lax.ppermute(edge_0, both, [(at(0, j), at(0, j ^ 1)) for j in early])
    edge_1 = pl.pallas_call(
        edge_kernel,
        out_shape=vds(S, H),
        in_specs=[VM] * 2,
        out_specs=VM,
        name="edge_1",
    )(flat(up_1), flat(down_1))
    corner_1 = lax.ppermute(
        edge_1,
        both,
        [(at(0, j), at(0, j ^ 1)) for j in late] + [(at(end, j), at(end, j ^ 1)) for j in range(nn)],
    )

    out = pl.pallas_call(
        final_kernel,
        out_shape=sds(S * 16, H),
        in_specs=[SM, SM] + [VM] * 19,
        out_specs=VM,
        scratch_shapes=[pltpu.SMEM((17,), jnp.int32), pltpu.VMEM((3 * SP, BURN_MAX * H), bf), vds(S, H)],
        name="step",
    )(
        ignited_stacks,
        spreading_number,
        x.reshape(S * 16, H),
        flat(up_0),
        flat(up_1),
        flat(down_0),
        flat(down_1),
        vmem(short),
        vmem(long_d),
        vmem(long_b),
        vmem(long_c),
        corner_below,
        corner_above,
        across_a,
        across_b,
        vmem(corner_0),
        vmem(corner_1),
        thermal_state.reshape(16, H),
        rate,
        left,
        right,
    )
    return out.reshape(S, 2, 8, H)


def solution(mesh):
    in_specs = (
        P(None, "wide", "narrow", None),
        P("wide", "narrow", None),
        P("wide", "narrow"),
        P(),
        P(),
        P(),
        P(),
        P(),
    )
    out_specs = P(None, "wide", "narrow", None)
    return jax.shard_map(shards, mesh=mesh, in_specs=in_specs, out_specs=out_specs, check_vma=False)
```
